256 devices in a mesh: mesh: 16 (over x_hi, y, core), tm: 16 (over z, x_lo).
Axes of the slice: x: 4 (x_hi: 2, x_lo: 2; x = x_hi * 2 + x_lo), y: 4, z: 8, core: 2. Of those that a mesh axis runs over, the one named last changes fastest.
Arguments:
- slice_start: float32 [16, 64, 128, 128], P('tm', 'mesh'), may hold values from -4 to 4
- conductivity: float32 [64, 128, 128], P('mesh'), may hold values from 0.5 to 2
- coil_current: float32 [64, 128, 128], P('mesh'), may hold values from -6 to 6
- switching: int32 [64], P('tm'), may hold values from -1 to 1
- loss_coeffs: float32 [3, 64, 128, 128], P(None, 'mesh', 'tm'), may hold values from 0.5 to 2
Outputs:
- next_start: float32 [16, 64, 128, 128], P('tm', 'mesh')
- loss_density: float32 [64, 128, 128], P('mesh', 'tm')
The draws below stay inside these ranges and needn't reach their ends.
All inputs are finite; a program needn't handle non-finite values.
Results may differ from the reference program's by a relative error of at most 0.000086.
Values sent between devices are 32-bit elements; how exact they have to be, the bound alone decides.
No kernel may reach another device: no remote copies, remote signals or barrier semaphores. Data moves between devices by JAX's collectives and lax.ppermute only.
A program may use at most 128 MiB of HBM per device.

```python
import math
import jax
import jax.numpy as jnp
from jax import lax

CZ = 128
STEPS = 4
SWEEPS = 5
CSWEEPS = 2
SLICES = 16
NX = 64
CY = 128
B = 64
H = 32


def touch_ends(entries, stream_key, low, largest):
    longest = entries.shape.index(max(entries.shape))
    spots = []
    for shift in (0, 1):
        where = [jax.random.randint(jax.random.fold_in(stream_key, axis), (), 0, length) for axis, length in enumerate(entries.shape)]
        where[longest] = (where[longest] + shift) % entries.shape[longest]
        spots.append(tuple(where))
    return entries.at[spots[0]].set(low).at[spots[1]].set(largest)


def block_scale(key, shape, split, smallest, high):
    def one(dim, parts):
        steps = jax.random.uniform(jax.random.fold_in(jax.random.fold_in(key, 6), dim), (parts,), jnp.float32, smallest / len(split), high / len(split))
        return jnp.repeat(jnp.exp(steps), shape[dim] // parts).reshape((-1,) + (1,) * (len(shape) - dim - 1))

    gain = one(*split[0])
    for cut in split[1:]:
        gain = gain * one(*cut)
    return gain


def bell_draw(rng, extent, spread, reach, pieces=(), held_as=jnp.bfloat16):
    values = spread * jax.random.normal(rng, extent, jnp.float32)
    if pieces:
        values = values * block_scale(rng, extent, pieces, -0.22, 0.18)
    return jnp.clip(values, -reach, reach).astype(held_as)


def setup_inputs(seed: int = 0) -> dict:
    keys = jax.random.split(jax.random.key(seed), 6)
    return {
        "slice_start": bell_draw(keys[0], (SLICES, NX, CY, CZ), 0.5, 4.0, ((0, 16), (1, 16)), jnp.float32),
        "conductivity": jnp.clip(jnp.exp(math.log(2.0) - 1.3862944 * jax.random.uniform(keys[1], (NX, CY, CZ), jnp.float32) ** block_scale(keys[1], (NX, CY, CZ), ((0, 16),), -0.2, 0.2)), 0.5, 2.0),
        "coil_current": bell_draw(keys[2], (NX, CY, CZ), 1.0, 6.0, ((0, 16),), jnp.float32),
        "switching": touch_ends(jax.random.randint(keys[3], (B,), -1, 2), jax.random.fold_in(keys[3], 1), -1, 1).astype(jnp.int32),
        "loss_coeffs": jnp.clip(jnp.exp(math.log(2.0) - 1.3862944 * jax.random.uniform(keys[4], (3, NX, CY, CZ), jnp.float32) ** block_scale(keys[4], (3, NX, CY, CZ), ((1, 16), (2, 16)), -0.2, 0.2)), 0.5, 2.0),
    }


time_step = 0.25


def chebyshev(apply_op, rhs, scale, sweeps):
    upper = 2.0 + 12.0 * scale
    center = (upper + 0.5) / 2.0
    radius = (upper - 0.5) / 2.0
    ratio = center / radius
    weight = 1.0 / ratio
    update = rhs / center
    result = update
    residual = rhs
    for sweep_index in range(sweeps):
        residual = residual - apply_op(update, scale)
        weight_next = 1.0 / (2.0 * ratio - weight)
        update = (weight_next * weight) * update + (2.0 * weight_next / radius) * residual
        result = result + update
        weight = weight_next
    return result


def z_difference(field):
    inner = field[..., 1:] - field[..., :-1]
    return jnp.concatenate([inner, jnp.zeros_like(field[..., :1])], axis=-1)


def dft_table(sample_times, total, harmonics):
    orders = jnp.arange(1, harmonics + 1, dtype=jnp.int32)
    product = (orders[:, None] * sample_times[None, :]) % total
    angle = (2.0 * jnp.pi / total) * product.astype(jnp.float32)
    return jnp.concatenate([jnp.cos(angle), -jnp.sin(angle)], axis=0)


def core_loss(spectrum, loss_coeffs, total):
    harmonics = total // 2
    real_part = spectrum[:harmonics]
    imag_part = spectrum[harmonics:]
    power = (real_part * real_part + imag_part * imag_part) * ((2.0 / total) ** 2)
    freq = (jnp.arange(1, harmonics + 1, dtype=jnp.int32).astype(jnp.float32) / harmonics).reshape(-1, 1, 1, 1)
    terms = loss_coeffs[0] * freq * power + loss_coeffs[1] * (freq * freq) * power
    terms = terms + loss_coeffs[2] * (freq ** 1.5) * (power ** 0.75)
    return jnp.sum(terms, axis=0)


def reference(slice_start, conductivity, coil_current, switching, loss_coeffs):
    def apply_op(field, scale):
        padded = jnp.pad(field, 1)
        beside = padded[2:, 1:-1, 1:-1] + padded[:-2, 1:-1, 1:-1]
        beside = beside + padded[1:-1, 2:, 1:-1] + padded[1:-1, :-2, 1:-1]
        beside = beside + padded[1:-1, 1:-1, 2:] + padded[1:-1, 1:-1, :-2]
        return conductivity * field + scale * (6.0 * field - beside)

    def coarse(field):
        return chebyshev(apply_op, conductivity * field, 4.0 * time_step, CSWEEPS)

    fluxes = []
    fine_ends = []
    jumps = []
    for slice_index in range(SLICES):
        state = slice_start[slice_index]
        for step_index in range(STEPS):
            level = switching[slice_index * STEPS + step_index].astype(jnp.float32)
            rhs = conductivity * state + time_step * level * coil_current
            state = chebyshev(apply_op, rhs, time_step, SWEEPS)
            fluxes.append(z_difference(state))
        fine_ends.append(state)
        jumps.append(state - coarse(slice_start[slice_index]))
    current = fine_ends[SLICES - 1]
    starts = [current]
    for slice_index in range(1, SLICES):
        current = coarse(current) + jumps[slice_index - 1]
        starts.append(current)
    next_start = jnp.stack(starts, axis=0)
    flux = jnp.stack(fluxes, axis=0)
    table = dft_table(jnp.arange(B, dtype=jnp.int32), B, H)
    spectrum = jnp.einsum('kt,txyz->kxyz', table, flux, precision=lax.Precision.HIGHEST)
    loss_density = core_loss(spectrum, loss_coeffs, B)
    return next_start, loss_density
```

```python
import functools

import jax
import jax.numpy as jnp
import numpy as np
from jax import lax
from jax.experimental import pallas as pl
from jax.experimental.pallas import tpu as pltpu
from jax.sharding import PartitionSpec as P

STEPS = 4
SWEEPS = 5
CSWEEPS = 2
TAU = 0.25
LINE = 16
ROWS = 8
NX = 64
CZ = 128
FINE_HALO = 5
S_HALO = 8

CHIP = [c if c < 4 else 11 - c for c in range(8)]
BLOCK_OF = [2 * CHIP[m // 2] + m % 2 for m in range(LINE)]
HOLDER = [BLOCK_OF.index(q) for q in range(LINE)]


def sweep_constants(scale, sweeps):
    upper = 2.0 + 12.0 * scale
    center = (upper + 0.5) / 2.0
    radius = (upper - 0.5) / 2.0
    ratio = center / radius
    weight = 1.0 / ratio
    pairs = []
    for _ in range(sweeps):
        weight_next = 1.0 / (2.0 * ratio - weight)
        pairs.append((weight_next * weight, 2.0 * weight_next / radius))
        weight = weight_next
    return 1.0 / center, pairs


def inside(block, row):
    place = block * ROWS + row
    return jnp.logical_and(place >= 0, place < LINE * ROWS)


def sweep(block, first_row, lo, hi, cond_at, rhs, old, now, scale, pair, first):
    alpha, beta = pair
    row_id = lax.broadcasted_iota(jnp.int32, (NX, CZ), 0)
    lane_id = lax.broadcasted_iota(jnp.int32, (NX, CZ), 1)
    own = 1.0 + alpha - 6.0 * scale * beta

    def body(row, carry):
        x = now[row]
        near = now[row - 1] + now[row + 1]
        near = near + jnp.where(row_id == 0, 0.0, pltpu.roll(x, 1, 0))
        near = near + jnp.where(row_id == NX - 1, 0.0, pltpu.roll(x, NX - 1, 0))
        near = near + jnp.where(lane_id == 0, 0.0, pltpu.roll(x, 1, 1))
        near = near + jnp.where(lane_id == CZ - 1, 0.0, pltpu.roll(x, CZ - 1, 1))
        gain = jnp.where(inside(block, first_row + row), beta * scale, 0.0)
        new = x * (own - beta * cond_at(row)) + beta * rhs[row] + gain * near
        if not first:
            new = new - alpha * old[row]
        old[row] = new
        return carry

    lax.fori_loop(lo, hi, body, 0)


def solve(block, first_row, lo, hi, cond_at, rhs, a, b, scale, sweeps):
    _, pairs = sweep_constants(scale, sweeps)
    old, now = b, a
    for k, pair in enumerate(pairs):
        sweep(block, first_row, lo + k + 1, hi - k - 1, cond_at, rhs, old, now, scale, pair, k == 0)
        old, now = now, old
    return now


def write_edges(parity, source, at, height, out_i, out_x):
    top = ROWS - height
    from_i = jnp.where(parity == 0, top, 0)
    out_i[...] = source[pl.ds(at + from_i, height)]
    out_x[...] = source[pl.ds(at + top - from_i, height)]


def spread(parity, target, height, own, halo_i, halo_x):
    far = height + ROWS
    place_i = jnp.where(parity == 0, far, 0)
    target[pl.ds(height, ROWS)] = own
    target[pl.ds(place_i, height)] = halo_i
    target[pl.ds(far - place_i, height)] = halo_x


def unpack_kernel(info, packed, cond, coil, start, edge_i, edge_x):
    for row in range(ROWS):
        for place, out in enumerate((cond, coil, start)):
            out[row] = packed[pl.ds(place * ROWS + row, NX, stride=3 * ROWS), :]
    parity = info[1]
    at = 0
    for out, height in ((cond, S_HALO), (coil, FINE_HALO), (start, FINE_HALO)):
        write_edges(parity, out, 0, height, edge_i.at[pl.ds(at, height)], edge_x.at[pl.ds(at, height)])
        at += height


def gather_kernel(info, cond, coil, halo_i, halo_x, cond_all, coil_all):
    parity = info[1]
    spread(parity, cond_all, S_HALO, cond[...], halo_i[pl.ds(0, S_HALO)], halo_x[pl.ds(0, S_HALO)])
    spread(
        parity,
        coil_all,
        FINE_HALO,
        coil[...],
        halo_i[pl.ds(S_HALO, FINE_HALO)],
        halo_x[pl.ds(S_HALO, FINE_HALO)],
    )


def fine_kernel(halo_at, step, info, cond, coil, own, halo_i, halo_x, state, sample, edge_i, edge_x, a, b, rhs):
    block, parity = info[0], info[1]
    height = FINE_HALO
    total = ROWS + 2 * height
    spread(parity, b, height, own[...], halo_i[pl.ds(halo_at, height)], halo_x[pl.ds(halo_at, height)])
    drive = TAU * info[3 + step].astype(jnp.float32)
    inverse, _ = sweep_constants(TAU, SWEEPS)
    shift = S_HALO - height

    def cond_at(row):
        return cond[row + shift]

    def start(row, carry):
        value = cond_at(row) * b[row] + drive * coil[row]
        rhs[row] = value
        a[row] = value * inverse
        return carry

    lax.fori_loop(0, total, start, 0)
    result = solve(block, -height, 0, total, cond_at, rhs, a, b, TAU, SWEEPS)
    for row in range(ROWS):
        value = result[height + row]
        state[row] = value
        sample[pl.ds(row, NX, stride=ROWS), :] = value
    write_edges(parity, result, height, height, edge_i, edge_x)


def coarse_kernel(power, info, cond, own, halo_i, halo_x, *rest):
    height = 2 * power
    outs, (a, b, rhs) = rest[:-3], rest[-3:]
    block, parity = info[0], info[1]
    total = ROWS + 2 * height
    spread(parity, a, height, own[...], halo_i[...], halo_x[...])
    scale = 4.0 * TAU
    inverse, _ = sweep_constants(scale, CSWEEPS)
    shift = S_HALO - height

    def cond_at(row):
        return cond[row + shift]

    lo, hi = 0, total
    value_in, spare = a, b
    for _ in range(power):

        def start(row, carry):
            value = cond_at(row) * value_in[row]
            rhs[row] = value
            value_in[row] = value * inverse
            return carry

        lax.fori_loop(lo, hi, start, 0)
        result = solve(block, -height, lo, hi, cond_at, rhs, value_in, spare, scale, CSWEEPS)
        spare = spare if result is value_in else value_in
        value_in = result
        lo, hi = lo + CSWEEPS, hi - CSWEEPS
    outs[0][...] = value_in[pl.ds(height, ROWS)]
    if len(outs) > 1:
        write_edges(parity, value_in, height, ROWS, outs[1], outs[2])


def combine_kernel(height, sign, info, left, right, out, edge_i, edge_x):
    out[...] = left[...] + sign * right[...]
    write_edges(info[1], out, 0, height, edge_i, edge_x)


def final_kernel(info, left, right, start, out):
    for row in range(ROWS):
        value = left[row] + right[row] + start[row]
        out[pl.ds(row, NX, stride=ROWS), :] = value


def shape(*dims):
    return jax.ShapeDtypeStruct(dims, jnp.float32)


def tile(rows=ROWS):
    return shape(rows, NX, CZ)


def call(kernel, name, outs, scratch, flops, *args):
    size = sum(int(np.prod(o.shape)) for o in outs) + sum(int(np.prod(a.shape)) for a in args[1:])
    return pl.pallas_call(
        kernel,
        out_shape=outs,
        in_specs=[pl.BlockSpec(memory_space=pltpu.SMEM)] + [pl.BlockSpec(memory_space=pltpu.VMEM)] * (len(args) - 1),
        out_specs=[pl.BlockSpec(memory_space=pltpu.VMEM)] * len(outs),
        scratch_shapes=[pltpu.VMEM((rows, NX, CZ), jnp.float32) for rows in scratch],
        cost_estimate=pl.CostEstimate(flops=flops, bytes_accessed=4 * size, transcendentals=0),
        compiler_params=pltpu.CompilerParams(vmem_limit_bytes=24 << 20),
        name=name,
    )(*args)


def swap_halos(edge_i, edge_x):
    inner = [(m, m ^ 1) for m in range(LINE)]
    outer = []
    for q in range(1, LINE - 1, 2):
        outer += [(HOLDER[q], HOLDER[q + 1]), (HOLDER[q + 1], HOLDER[q])]
    return lax.ppermute(edge_i, "mesh", inner), lax.ppermute(edge_x, "mesh", outer)


def later(value, distance, cyclic=False):
    route = [(n, (n + distance) % LINE) for n in range(LINE) if cyclic or n + distance < LINE]
    return lax.ppermute(value, "tm", route)


def dft_table(sample_times, total, harmonics):
    orders = jnp.arange(1, harmonics + 1, dtype=jnp.int32)
    product = orders[:, None] * sample_times[None, :] % total
    angle = 2.0 * jnp.pi / total * product.astype(jnp.float32)
    return jnp.concatenate([jnp.cos(angle), -jnp.sin(angle)], axis=0)


def z_difference(field):
    inner = field[..., 1:] - field[..., :-1]
    return jnp.concatenate([inner, jnp.zeros_like(field[..., :1])], axis=-1)


def core_loss(spectrum, loss_coeffs, total):
    harmonics = total // 2
    real_part = spectrum[:harmonics]
    imag_part = spectrum[harmonics:]
    power = (real_part * real_part + imag_part * imag_part) * (2.0 / total) ** 2
    freq = (jnp.arange(1, harmonics + 1, dtype=jnp.int32).astype(jnp.float32) / harmonics).reshape(-1, 1, 1, 1)
    root = jnp.sqrt(power)
    terms = loss_coeffs[0] * freq * power + loss_coeffs[1] * (freq * freq) * power
    terms = terms + loss_coeffs[2] * freq**1.5 * (root * jnp.sqrt(root))
    return jnp.sum(terms, axis=0)


def on_device(slice_start, conductivity, coil_current, switching, loss_coeffs):
    total = STEPS * LINE
    block = jnp.asarray(BLOCK_OF, jnp.int32)[lax.axis_index("mesh")]
    info = jnp.concatenate([jnp.stack([block, block % 2, block]), switching]).astype(jnp.int32)

    fields = jnp.stack([conductivity, coil_current, slice_start[0]], axis=1)
    fields = fields.reshape(4, 3, LINE, ROWS, CZ)
    fields = jnp.stack([fields[:, :, q] for q in BLOCK_OF], axis=0)
    packed = lax.all_to_all(fields, "mesh", 0, 0, tiled=True).reshape(LINE * 4 * 3 * ROWS, CZ)

    to_spectrum = [(m * LINE + t, HOLDER[t] * LINE + m) for m in range(LINE) for t in range(LINE)]
    back = [(target, source) for source, target in to_spectrum]
    coeffs = lax.ppermute(loss_coeffs, ("mesh", "tm"), to_spectrum)

    edge_rows = S_HALO + 2 * FINE_HALO
    cond, coil, start, edge_i, edge_x = call(
        unpack_kernel, "unpack", [tile(), tile(), tile(), tile(edge_rows), tile(edge_rows)], [], 0, info, packed
    )
    halo_i, halo_x = swap_halos(edge_i, edge_x)
    cond_all, coil_all = call(
        gather_kernel,
        "gather",
        [tile(ROWS + 2 * S_HALO), tile(ROWS + 2 * FINE_HALO)],
        [],
        0,
        info,
        cond,
        coil,
        halo_i,
        halo_x,
    )
    state, samples = start, []
    rows = ROWS + 2 * FINE_HALO
    for step in range(STEPS):
        state, sample, edge_i, edge_x = call(
            functools.partial(fine_kernel, S_HALO + FINE_HALO if step == 0 else 0, step),
            "fine",
            [tile(), shape(NX * ROWS, CZ), tile(FINE_HALO), tile(FINE_HALO)],
            [rows] * 3,
            20 * SWEEPS * rows * NX * CZ,
            info,
            cond_all,
            coil_all,
            state,
            halo_i,
            halo_x,
        )
        samples.append(sample.reshape(LINE, 4, ROWS, CZ))
        if step + 1 < STEPS:
            halo_i, halo_x = swap_halos(edge_i, edge_x)

    arrived = later(state, 1, cyclic=True)
    other, sign = start, -1.0
    value = arrived
    for power in (1, 2, 4, 8):
        height = min(2 * power, S_HALO)
        value, edge_i, edge_x = call(
            functools.partial(combine_kernel, height, sign),
            "combine",
            [tile(), tile(height), tile(height)],
            [],
            0,
            info,
            value,
            other,
        )
        sign = 1.0
        moved = value
        halves = max(1, power // 4)
        for half in range(halves):
            halo_i, halo_x = swap_halos(edge_i, edge_x)
            own_power = power // halves
            more = half + 1 < halves
            rows = ROWS + 2 * height
            result = call(
                functools.partial(coarse_kernel, own_power),
                "coarse",
                [tile()] + ([tile(), tile()] if more else []),
                [rows] * 3,
                20 * CSWEEPS * own_power * rows * NX * CZ,
                info,
                cond_all,
                moved,
                halo_i,
                halo_x,
            )
            moved = result[0]
            if more:
                edge_i, edge_x = result[1], result[2]
        other = later(moved, power)
    (out,) = call(final_kernel, "final", [shape(NX * ROWS, CZ)], [], 0, info, value, other, start)
    out = lax.all_to_all(out.reshape(LINE, 4, ROWS, CZ), "mesh", 0, 0, tiled=True)
    next_start = jnp.stack([out[m] for m in HOLDER], axis=1).reshape(1, 4, LINE * ROWS, CZ)

    gathered = jnp.stack(samples, axis=1)
    gathered = lax.all_to_all(gathered, "tm", 0, 0, tiled=True).reshape(total, 4, ROWS, CZ)
    table = dft_table(jnp.arange(total, dtype=jnp.int32), total, total // 2)
    spectrum = jnp.einsum("kt,txyz->kxyz", table, z_difference(gathered), precision=lax.Precision.HIGHEST)
    loss = core_loss(spectrum, coeffs, total)
    loss_density = lax.ppermute(loss, ("mesh", "tm"), back)
    return next_start, loss_density


def solution(mesh):
    placed = (
        P("tm", "mesh", None, None),
        P("mesh", None, None),
        P("mesh", None, None),
        P("tm"),
        P(None, "mesh", "tm", None),
    )
    return jax.shard_map(
        on_device,
        mesh=mesh,
        in_specs=placed,
        out_specs=(P("tm", "mesh", None, None), P("mesh", "tm", None)),
        check_vma=False,
    )
```

```python
import functools

import jax
import jax.numpy as jnp
import numpy as np
from jax import lax
from jax.experimental import pallas as pl
from jax.experimental.pallas import tpu as pltpu
from jax.sharding import PartitionSpec as P


STEPS = 4
SWEEPS = 5
CSWEEPS = 2
TAU = 0.25
LINE = 16
ROWS = 8
NX = 64
CZ = 128
FINE_HALO = 5
S_HALO = 8

CHIP = [c if c < 4 else 11 - c for c in range(8)]
BLOCK_OF = [2 * CHIP[m // 2] + m % 2 for m in range(LINE)]
HOLDER = [BLOCK_OF.index(q) for q in range(LINE)]


def sweep_constants(scale, sweeps):
    upper = 2.0 + 12.0 * scale
    center = (upper + 0.5) / 2.0
    radius = (upper - 0.5) / 2.0
    ratio = center / radius
    weight = 1.0 / ratio
    pairs = []
    for _ in range(sweeps):
        weight_next = 1.0 / (2.0 * ratio - weight)
        pairs.append((weight_next * weight, 2.0 * weight_next / radius))
        weight = weight_next
    return 1.0 / center, pairs


def near_sum(now, row):
    row_id = lax.broadcasted_iota(jnp.int32, (NX, CZ), 0)
    lane_id = lax.broadcasted_iota(jnp.int32, (NX, CZ), 1)
    x = now[row]
    near = now[row - 1] + now[row + 1]
    near = near + jnp.where(row_id == 0, 0.0, pltpu.roll(x, 1, 0))
    near = near + jnp.where(row_id == NX - 1, 0.0, pltpu.roll(x, NX - 1, 0))
    near = near + jnp.where(lane_id == 0, 0.0, pltpu.roll(x, 1, 1))
    near = near + jnp.where(lane_id == CZ - 1, 0.0, pltpu.roll(x, CZ - 1, 1))
    return x, near


def solve(block, height, lo, hi, cond_at, rhs, a, b, scale, sweeps, store):
    inverse, pairs = sweep_constants(scale, sweeps)
    low = jnp.where(block > 0, 1.0, 0.0)
    high = jnp.where(block < LINE - 1, 1.0, 0.0)
    old, now = None, None
    for k, (alpha, beta) in enumerate(pairs):
        own = 1.0 + alpha - 6.0 * scale * beta
        unit = inverse if k == 0 else 1.0
        target = (a, b)[k % 2]
        for row in range(lo + k + 1, hi - k - 1):
            gain = unit * beta * scale
            if row < height:
                gain = gain * low
            elif row >= height + ROWS:
                gain = gain * high
            if k == 0:
                x, near = near_sum(rhs, row)
                new = x * ((inverse * own + beta) - (inverse * beta) * cond_at(row)) + gain * near
            else:
                x, near = near_sum(now, row)
                new = x * (own - beta * cond_at(row)) + gain * near
                if k == 1:
                    new = new + (beta - alpha * inverse) * rhs[row]
                else:
                    new = new + beta * rhs[row] - alpha * old[row]
            if k == sweeps - 1:
                store(row, new)
            else:
                target[row] = new
        old, now = now, target


def write_edges(parity, source, at, height, out_i, out_x):
    top = ROWS - height
    from_i = jnp.where(parity == 0, top, 0)
    out_i[...] = source[pl.ds(at + from_i, height)]
    out_x[...] = source[pl.ds(at + top - from_i, height)]


def places(parity, height):
    far = height + ROWS
    place_i = jnp.where(parity == 0, far, 0)
    return place_i, far - place_i


def pack_kernel(cond, coil, start, out, sems):
    copies = []
    for place, field in enumerate((cond, coil, start)):
        for m in range(LINE):
            copies.append(
                pltpu.make_async_copy(
                    field.at[:, pl.ds(BLOCK_OF[m] * ROWS, ROWS), :], out.at[m, :, place], sems.at[place * LINE + m]
                )
            )
    for copy in copies:
        copy.start()
    for copy in copies:
        copy.wait()


def unpack_kernel(info, packed, cond, coil, start, edge_i, edge_x):
    for row in range(ROWS):
        for place, out in enumerate((cond, coil, start)):
            out[row] = packed[pl.ds(place * ROWS + row, NX, stride=3 * ROWS), :]
    parity = info[1]
    at = 0
    for out, height in ((cond, S_HALO), (coil, FINE_HALO), (start, FINE_HALO)):
        write_edges(parity, out, 0, height, edge_i.at[pl.ds(at, height)], edge_x.at[pl.ds(at, height)])
        at += height


def gather_kernel(info, cond, coil, halo_i, halo_x, cond_all, coil_all):
    at = 0
    for own, target, height in ((cond, cond_all, S_HALO), (coil, coil_all, FINE_HALO)):
        place_i, place_x = places(info[1], height)
        target[pl.ds(height, ROWS)] = own[...]
        target[pl.ds(place_i, height)] = halo_i[pl.ds(at, height)]
        target[pl.ds(place_x, height)] = halo_x[pl.ds(at, height)]
        at += height


def first_kernel(info, cond, coil, own, halo_i, halo_x, state, edge_i, edge_x, cond_all, coil_all, a, b, rhs):
    gather_kernel(info, cond, coil, halo_i, halo_x, cond_all, coil_all)
    fine_kernel(
        S_HALO + FINE_HALO, 0, info, cond_all, coil_all, own, halo_i, halo_x, state, edge_i, edge_x, a, b, rhs
    )


def fine_kernel(halo_at, step, info, cond, coil, own, halo_i, halo_x, state, edge_i, edge_x, a, b, rhs):
    block, parity = info[0], info[1]
    height = FINE_HALO
    total = ROWS + 2 * height
    drive = TAU * info[3 + step].astype(jnp.float32)
    shift = S_HALO - height
    place_i, place_x = places(parity, height)
    for at, size, field, start in (
        (height, ROWS, own, 0),
        (place_i, height, halo_i, halo_at),
        (place_x, height, halo_x, halo_at),
    ):
        for row in range(size):
            rhs[at + row] = cond[at + row + shift] * field[start + row] + drive * coil[at + row]

    def store(row, value):
        state[row - height] = value

    solve(block, height, 0, total, lambda row: cond[row + shift], rhs, a, b, TAU, SWEEPS, store)
    write_edges(parity, state, 0, height, edge_i, edge_x)


def coarse_kernel(power, height, halo_at, info, cond, own, halo_i, halo_x, *rest):
    outs, (a, b, c) = rest[:-3], rest[-3:]
    block, parity = info[0], info[1]
    scale = 4.0 * TAU
    shift = S_HALO - height
    place_i, place_x = places(parity, height)
    for at, size, field, start in (
        (height, ROWS, own, 0),
        (place_i, height, halo_i, halo_at),
        (place_x, height, halo_x, halo_at),
    ):
        for row in range(size):
            a[at + row] = cond[at + row + shift] * field[start + row]
    lo, hi = height - CSWEEPS * power, height + ROWS + CSWEEPS * power
    rhs, result = a, c
    for turn in range(power):
        if turn + 1 < power:

            def store(row, value, result=result):
                result[row] = cond[row + shift] * value

        else:

            def store(row, value):
                outs[0][row - height] = value

        solve(block, height, lo, hi, lambda row: cond[row + shift], rhs, b, None, scale, CSWEEPS, store)
        rhs, result = result, rhs
        lo, hi = lo + CSWEEPS, hi - CSWEEPS
    if len(outs) > 1:
        write_edges(parity, outs[0], 0, ROWS, outs[1], outs[2])


def combine_kernel(height, first, info, left, right, out, edge_i, edge_x):
    value = right[...]
    if first:
        value = value * jnp.where(info[2] == LINE - 1, 0.0, -1.0)
    out[...] = left[...] + value
    write_edges(info[1], out, 0, height, edge_i, edge_x)


def columns_kernel(*refs):
    fields, out = refs[:-1], refs[-1]
    for row in range(ROWS):
        for place, field in enumerate(fields):
            value = field[row]
            for m in range(LINE):
                first = (m * len(fields) + place) * (NX // LINE) * ROWS
                out[pl.ds(first + row, NX // LINE, stride=ROWS), :] = value[m * 4 : m * 4 + 4]


def final_kernel(left, right, out):
    for row in range(ROWS):
        out[pl.ds(row, NX, stride=ROWS), :] = left[row] + right[row]


def lay_out_kernel(blocks, out, sems):
    copies = []
    for m in range(LINE):
        target = out.at[0, :, pl.ds(BLOCK_OF[m] * ROWS, ROWS), :]
        copies.append(pltpu.make_async_copy(blocks.at[m], target, sems.at[m]))
    for copy in copies:
        copy.start()
    for copy in copies:
        copy.wait()


def move(kernel, out, count, from_hbm, to_hbm, *args):
    source = pltpu.HBM if from_hbm else pltpu.VMEM
    return pl.pallas_call(
        kernel,
        out_shape=out,
        in_specs=[pl.BlockSpec(memory_space=source)] * len(args),
        out_specs=pl.BlockSpec(memory_space=pltpu.HBM if to_hbm else pltpu.VMEM),
        scratch_shapes=[pltpu.SemaphoreType.DMA((count,))],
        compiler_params=pltpu.CompilerParams(vmem_limit_bytes=60 << 20),
    )(*args)


def shape(*dims):
    return jax.ShapeDtypeStruct(dims, jnp.float32)


def tile(rows=ROWS):
    return shape(rows, NX, CZ)


def call(kernel, outs, scratch, flops, *args):
    size = sum(int(np.prod(o.shape)) for o in outs) + sum(int(np.prod(a.shape)) for a in args)
    spaces = [pltpu.SMEM if a.dtype == jnp.int32 else pltpu.VMEM for a in args]
    return pl.pallas_call(
        kernel,
        out_shape=outs,
        in_specs=[pl.BlockSpec(memory_space=space) for space in spaces],
        out_specs=[pl.BlockSpec(memory_space=pltpu.VMEM)] * len(outs),
        scratch_shapes=[pltpu.VMEM((rows, NX, CZ), jnp.float32) for rows in scratch],
        cost_estimate=pl.CostEstimate(flops=flops, bytes_accessed=4 * size, transcendentals=0),
        compiler_params=pltpu.CompilerParams(vmem_limit_bytes=24 << 20),
    )(*args)


def swap_halos(edge_i, edge_x):
    inner = [(m, m ^ 1) for m in range(LINE)]
    outer = []
    for q in range(1, LINE - 1, 2):
        outer += [(HOLDER[q], HOLDER[q + 1]), (HOLDER[q + 1], HOLDER[q])]
    halo_x = lax.ppermute(edge_x, "mesh", outer)
    halo_i = lax.ppermute(edge_i, "mesh", inner)
    return halo_i, halo_x


def later(value, distance, shift=0):
    route = [((p - 1) % LINE, (p + distance - 1 + shift) % LINE) for p in range(LINE) if p + distance < LINE]
    return lax.ppermute(value, "tm", route)


def dft_table(sample_times, total, harmonics):
    orders = jnp.arange(1, harmonics + 1, dtype=jnp.int32)
    product = orders[:, None] * sample_times[None, :] % total
    angle = 2.0 * jnp.pi / total * product.astype(jnp.float32)
    return jnp.concatenate([jnp.cos(angle), -jnp.sin(angle)], axis=0)


def z_difference(field):
    inner = field[..., 1:] - field[..., :-1]
    return jnp.concatenate([inner, jnp.zeros_like(field[..., :1])], axis=-1)


def loss_sums(spectrum, total):
    harmonics = total // 2
    real_part = spectrum[:harmonics]
    imag_part = spectrum[harmonics:]
    power = (real_part * real_part + imag_part * imag_part) * (2.0 / total) ** 2
    freq = (jnp.arange(1, harmonics + 1, dtype=jnp.int32).astype(jnp.float32) / harmonics).reshape(-1, 1, 1, 1)
    root = jnp.sqrt(power)
    terms = (freq * power, (freq * freq) * power, freq**1.5 * (root * jnp.sqrt(root)))
    return jnp.stack([jnp.sum(term, axis=0) for term in terms], axis=0)


def by_cell(states):
    count = len(states)
    (packed,) = call(columns_kernel, [shape(LINE * count * 4 * ROWS, CZ)], [], 0, *states)
    packed = lax.all_to_all(packed.reshape(LINE, count, 4, ROWS, CZ), "tm", 0, 0, tiled=True)
    return packed.reshape(LINE * count, 4, ROWS, CZ)


def iteration(slice_start, conductivity, coil_current, switching, loss_coeffs):
    total = STEPS * LINE
    block = jnp.asarray(BLOCK_OF, jnp.int32)[lax.axis_index("mesh")]
    info = jnp.concatenate([jnp.stack([block, block % 2, lax.axis_index("tm")]), switching]).astype(jnp.int32)

    fields = move(
        pack_kernel, shape(LINE, 4, 3, ROWS, CZ), 3 * LINE, True, False, conductivity, coil_current, slice_start[0]
    )
    packed = lax.all_to_all(fields, "mesh", 0, 0, tiled=True)

    packed = packed.reshape(LINE * 4 * 3 * ROWS, CZ)

    edge_rows = S_HALO + 2 * FINE_HALO
    cond, coil, start, edge_i, edge_x = call(
        unpack_kernel, [tile(), tile(), tile(), tile(edge_rows), tile(edge_rows)], [], 0, info, packed
    )
    rows = ROWS + 2 * FINE_HALO
    halo_i, halo_x = first_i, first_x = swap_halos(edge_i, edge_x)
    state, edge_i, edge_x, cond_all, coil_all = call(
        first_kernel,
        [tile(), tile(FINE_HALO), tile(FINE_HALO), tile(ROWS + 2 * S_HALO), tile(rows)],
        [rows] * 3,
        20 * SWEEPS * rows * NX * CZ,
        info,
        cond,
        coil,
        start,
        halo_i,
        halo_x,
    )

    def coarse(power, height, halo_at, value, halo_i, halo_x, edges=0):
        rows = ROWS + 2 * height
        return call(
            functools.partial(coarse_kernel, power, height, halo_at),
            [tile()] + [tile()] * edges,
            [rows] * 3,
            20 * CSWEEPS * power * rows * NX * CZ,
            info,
            cond_all,
            value,
            halo_i,
            halo_x,
        )

    (coarse_start,) = coarse(1, FINE_HALO, S_HALO + FINE_HALO, start, first_i, first_x)
    states = [state]
    for step in range(1, STEPS):
        halo_i, halo_x = swap_halos(edge_i, edge_x)
        if step == STEPS - 1:
            early = by_cell(states)
        state, edge_i, edge_x = call(
            functools.partial(fine_kernel, 0, step),
            [tile(), tile(FINE_HALO), tile(FINE_HALO)],
            [rows] * 3,
            20 * SWEEPS * rows * NX * CZ,
            info,
            cond_all,
            coil_all,
            state,
            halo_i,
            halo_x,
        )
        states.append(state)
    value, other = state, coarse_start
    for power in (1, 2, 4):
        value, edge_i, edge_x = call(
            functools.partial(combine_kernel, 2 * power, power == 1),
            [tile(), tile(2 * power), tile(2 * power)],
            [],
            0,
            info,
            value,
            other,
        )
        halo_i, halo_x = swap_halos(edge_i, edge_x)
        (moved,) = coarse(power, 2 * power, 0, value, halo_i, halo_x)
        other = later(moved, power)
    value, edge_i, edge_x = call(
        functools.partial(combine_kernel, ROWS, False), [tile()] * 3, [], 0, info, value, other
    )
    value, edge_i, edge_x, late = lax.optimization_barrier((value, edge_i, edge_x, states[-1]))
    final = by_cell([late])
    table = dft_table(jnp.arange(total, dtype=jnp.int32), total, total // 2).reshape(total, LINE, STEPS)
    first_steps = table[:, :, : STEPS - 1].reshape(total, -1)
    spectrum = jnp.einsum("kt,txyz->kxyz", first_steps, z_difference(early), precision=lax.Precision.HIGHEST)
    last_step = table[:, :, STEPS - 1]
    spectrum += jnp.einsum("kt,txyz->kxyz", last_step, z_difference(final), precision=lax.Precision.HIGHEST)
    sums = loss_sums(spectrum, total)

    left = later(value, 0, shift=1)
    halo_i, halo_x = swap_halos(edge_i, edge_x)
    moved, edge_i, edge_x = coarse(4, ROWS, 0, value, halo_i, halo_x, edges=2)
    halo_i, halo_x = swap_halos(edge_i, edge_x)
    (moved,) = coarse(4, ROWS, 0, moved, halo_i, halo_x)
    right = later(moved, 8, shift=1)
    right, sums = lax.optimization_barrier((right, sums))
    (out,) = call(final_kernel, [shape(NX * ROWS, CZ)], [], 0, left, right)
    out = lax.all_to_all(out.reshape(LINE, 4, ROWS, CZ), "mesh", 0, 0, tiled=True)
    route = [(m * LINE + t, t * LINE + BLOCK_OF[m]) for m in range(LINE) for t in range(LINE)]
    sums = lax.ppermute(sums, ("mesh", "tm"), route)
    loss_density = jnp.sum(loss_coeffs * sums, axis=0)
    next_start = move(lay_out_kernel, shape(1, 4, LINE * ROWS, CZ), LINE, False, True, out)
    return next_start, loss_density


def solution(mesh):
    placed = (
        P("tm", "mesh", None, None),
        P("mesh", None, None),
        P("mesh", None, None),
        P("tm"),
        P(None, "mesh", "tm", None),
    )
    return jax.shard_map(
        iteration,
        mesh=mesh,
        in_specs=placed,
        out_specs=(P("tm", "mesh", None, None), P("mesh", "tm", None)),
        check_vma=False,
    )
```

```python
import functools

import jax
import jax.numpy as jnp
import numpy as np
from jax import lax
from jax.experimental import pallas as pl
from jax.experimental.pallas import tpu as pltpu
from jax.sharding import PartitionSpec as P


STEPS = 4
SWEEPS = 5
CSWEEPS = 2
TAU = 0.25
LINE = 16
ROWS = 8
NX = 64
CZ = 128
FINE_HALO = 5
S_HALO = 8
DISTANCES = (8, 4, 2, 1)

CHIP = [c if c < 4 else 11 - c for c in range(8)]
BLOCK_OF = [2 * CHIP[m // 2] + m % 2 for m in range(LINE)]
HOLDER = [BLOCK_OF.index(q) for q in range(LINE)]


def sweep_constants(scale, sweeps):
    upper = 2.0 + 12.0 * scale
    center = (upper + 0.5) / 2.0
    radius = (upper - 0.5) / 2.0
    ratio = center / radius
    weight = 1.0 / ratio
    pairs = []
    for _ in range(sweeps):
        weight_next = 1.0 / (2.0 * ratio - weight)
        pairs.append((weight_next * weight, 2.0 * weight_next / radius))
        weight = weight_next
    return 1.0 / center, pairs


def near_sum(now, row):
    row_id = lax.broadcasted_iota(jnp.int32, (NX, CZ), 0)
    lane_id = lax.broadcasted_iota(jnp.int32, (NX, CZ), 1)
    x = now[row]
    near = now[row - 1] + now[row + 1]
    near = near + jnp.where(row_id == 0, 0.0, pltpu.roll(x, 1, 0))
    near = near + jnp.where(row_id == NX - 1, 0.0, pltpu.roll(x, NX - 1, 0))
    near = near + jnp.where(lane_id == 0, 0.0, pltpu.roll(x, 1, 1))
    near = near + jnp.where(lane_id == CZ - 1, 0.0, pltpu.roll(x, CZ - 1, 1))
    return x, near


def solve(block, height, lo, hi, cond_at, rhs, a, b, scale, sweeps, store):
    inverse, pairs = sweep_constants(scale, sweeps)
    low = jnp.where(block > 0, 1.0, 0.0)
    high = jnp.where(block < LINE - 1, 1.0, 0.0)
    old, now = None, None
    for k, (alpha, beta) in enumerate(pairs):
        own = 1.0 + alpha - 6.0 * scale * beta
        unit = inverse if k == 0 else 1.0
        target = (a, b)[k % 2]
        for row in range(lo + k + 1, hi - k - 1):
            gain = unit * beta * scale
            if row < height:
                gain = gain * low
            elif row >= height + ROWS:
                gain = gain * high
            if k == 0:
                x, near = near_sum(rhs, row)
                new = x * ((inverse * own + beta) - (inverse * beta) * cond_at(row)) + gain * near
            else:
                x, near = near_sum(now, row)
                new = x * (own - beta * cond_at(row)) + gain * near
                if k == 1:
                    new = new + (beta - alpha * inverse) * rhs[row]
                else:
                    new = new + beta * rhs[row] - alpha * old[row]
            if k == sweeps - 1:
                store(row, new)
            else:
                target[row] = new
        old, now = now, target


def write_edges(parity, source, at, height, out_i, out_x):
    top = ROWS - height
    from_i = jnp.where(parity == 0, top, 0)
    out_i[...] = source[pl.ds(at + from_i, height)]
    out_x[...] = source[pl.ds(at + top - from_i, height)]


def places(parity, height):
    far = height + ROWS
    place_i = jnp.where(parity == 0, far, 0)
    return place_i, far - place_i


def pack_kernel(cond, coil, start, out, sems):
    copies = []
    for place, field in enumerate((cond, coil, start)):
        for m in range(LINE):
            copies.append(
                pltpu.make_async_copy(
                    field.at[:, pl.ds(BLOCK_OF[m] * ROWS, ROWS), :], out.at[m, :, place], sems.at[place * LINE + m]
                )
            )
    for copy in copies:
        copy.start()
    for copy in copies:
        copy.wait()


def unpack_kernel(info, packed, cond, coil, start, edge_i, edge_x):
    for row in range(ROWS):
        for place, out in enumerate((cond, coil, start)):
            out[row] = packed[pl.ds(place * ROWS + row, NX, stride=3 * ROWS), :]
    parity = info[1]
    at = 0
    for out, height in ((cond, S_HALO), (coil, FINE_HALO), (start, FINE_HALO)):
        write_edges(parity, out, 0, height, edge_i.at[pl.ds(at, height)], edge_x.at[pl.ds(at, height)])
        at += height


def gather_kernel(info, cond, coil, halo_i, halo_x, cond_all, coil_all):
    at = 0
    for own, target, height in ((cond, cond_all, S_HALO), (coil, coil_all, FINE_HALO)):
        place_i, place_x = places(info[1], height)
        target[pl.ds(height, ROWS)] = own[...]
        target[pl.ds(place_i, height)] = halo_i[pl.ds(at, height)]
        target[pl.ds(place_x, height)] = halo_x[pl.ds(at, height)]
        at += height


def first_kernel(info, cond, coil, own, halo_i, halo_x, state, edge_i, edge_x, cond_all, coil_all, a, b, rhs):
    gather_kernel(info, cond, coil, halo_i, halo_x, cond_all, coil_all)
    fine_kernel(
        S_HALO + FINE_HALO, 0, info, cond_all, coil_all, own, halo_i, halo_x, state, edge_i, edge_x, a, b, rhs
    )


def fine_kernel(halo_at, step, info, cond, coil, own, halo_i, halo_x, state, edge_i, edge_x, a, b, rhs):
    block, parity = info[0], info[1]
    height = FINE_HALO
    total = ROWS + 2 * height
    drive = TAU * info[3 + step].astype(jnp.float32)
    shift = S_HALO - height
    place_i, place_x = places(parity, height)
    for at, size, field, start in (
        (height, ROWS, own, 0),
        (place_i, height, halo_i, halo_at),
        (place_x, height, halo_x, halo_at),
    ):
        for row in range(size):
            rhs[at + row] = cond[at + row + shift] * field[start + row] + drive * coil[at + row]

    def store(row, value):
        state[row - height] = value

    solve(block, height, 0, total, lambda row: cond[row + shift], rhs, a, b, TAU, SWEEPS, store)
    write_edges(parity, state, 0, height, edge_i, edge_x)


def coarse_kernel(power, height, halo_at, info, cond, own, halo_i, halo_x, *rest):
    outs, (a, b, c) = rest[:-3], rest[-3:]
    block, parity = info[0], info[1]
    scale = 4.0 * TAU
    shift = S_HALO - height
    place_i, place_x = places(parity, height)
    for at, size, field, start in (
        (height, ROWS, own, 0),
        (place_i, height, halo_i, halo_at),
        (place_x, height, halo_x, halo_at),
    ):
        for row in range(size):
            a[at + row] = cond[at + row + shift] * field[start + row]
    lo, hi = height - CSWEEPS * power, height + ROWS + CSWEEPS * power
    rhs, result = a, c
    for turn in range(power):
        if turn + 1 < power:

            def store(row, value, result=result):
                result[row] = cond[row + shift] * value

        else:

            def store(row, value):
                outs[0][row - height] = value

        solve(block, height, lo, hi, lambda row: cond[row + shift], rhs, b, None, scale, CSWEEPS, store)
        rhs, result = result, rhs
        lo, hi = lo + CSWEEPS, hi - CSWEEPS
    if len(outs) > 1:
        write_edges(parity, outs[0], 0, ROWS, outs[1], outs[2])


def reaches(info, distance, moved):
    position = lax.rem(info[2] + 1 + moved, LINE)
    return jnp.where(position + distance < LINE, 1.0, 0.0)


def jump_kernel(height, info, fine_end, coarse_start, out, edge_i, edge_x):
    out[...] = fine_end[...] - jnp.where(info[2] == LINE - 1, 0.0, 1.0) * coarse_start[...]
    write_edges(info[1], out, 0, height, edge_i, edge_x)


def combine_kernel(height, distance, moved, info, arrived, product, out, edge_i, edge_x):
    out[...] = arrived[...] + reaches(info, distance, moved) * product[...]
    write_edges(info[1], out, 0, height, edge_i, edge_x)


def columns_kernel(*refs):
    fields, out = refs[:-1], refs[-1]
    for row in range(ROWS):
        for place, field in enumerate(fields):
            value = field[row]
            for m in range(LINE):
                first = (m * len(fields) + place) * (NX // LINE) * ROWS
                out[pl.ds(first + row, NX // LINE, stride=ROWS), :] = value[m * 4 : m * 4 + 4]


def final_kernel(distance, moved, info, arrived, product, out):
    factor = reaches(info, distance, moved)
    for row in range(ROWS):
        out[pl.ds(row, NX, stride=ROWS), :] = arrived[row] + factor * product[row]


def lay_out_kernel(blocks, out):
    for m in range(LINE):
        for x in range(NX // LINE):
            out[0, x, pl.ds(BLOCK_OF[m] * ROWS, ROWS), :] = blocks[m, x]


def gathered_copies(kernel, out, count, *args):
    return pl.pallas_call(
        kernel,
        out_shape=out,
        in_specs=[pl.BlockSpec(memory_space=pltpu.HBM)] * len(args),
        out_specs=pl.BlockSpec(memory_space=pltpu.VMEM),
        scratch_shapes=[pltpu.SemaphoreType.DMA((count,))],
        compiler_params=pltpu.CompilerParams(vmem_limit_bytes=60 << 20),
    )(*args)


def shape(*dims):
    return jax.ShapeDtypeStruct(dims, jnp.float32)


def tile(rows=ROWS):
    return shape(rows, NX, CZ)


def call(kernel, outs, scratch, flops, *args):
    size = sum(int(np.prod(o.shape)) for o in outs) + sum(int(np.prod(a.shape)) for a in args)
    spaces = [pltpu.SMEM if a.dtype == jnp.int32 else pltpu.VMEM for a in args]
    return pl.pallas_call(
        kernel,
        out_shape=outs,
        in_specs=[pl.BlockSpec(memory_space=space) for space in spaces],
        out_specs=[pl.BlockSpec(memory_space=pltpu.VMEM)] * len(outs),
        scratch_shapes=[pltpu.VMEM((rows, NX, CZ), jnp.float32) for rows in scratch],
        cost_estimate=pl.CostEstimate(flops=flops, bytes_accessed=4 * size, transcendentals=0),
        compiler_params=pltpu.CompilerParams(vmem_limit_bytes=24 << 20),
    )(*args)


def swap_halos(edge_i, edge_x):
    inner = [(m, m ^ 1) for m in range(LINE)]
    outer = []
    for q in range(1, LINE - 1, 2):
        outer += [(HOLDER[q], HOLDER[q + 1]), (HOLDER[q + 1], HOLDER[q])]
    halo_x = lax.ppermute(edge_x, "mesh", outer)
    halo_i = lax.ppermute(edge_i, "mesh", inner)
    return halo_i, halo_x


def earlier(value, distance):
    return lax.ppermute(value, "tm", [(n, (n - distance) % LINE) for n in range(LINE)])


def dft_table(sample_times, total, harmonics):
    orders = jnp.arange(1, harmonics + 1, dtype=jnp.int32)
    product = orders[:, None] * sample_times[None, :] % total
    angle = 2.0 * jnp.pi / total * product.astype(jnp.float32)
    return jnp.concatenate([jnp.cos(angle), -jnp.sin(angle)], axis=0)


def z_difference(field):
    inner = field[..., 1:] - field[..., :-1]
    return jnp.concatenate([inner, jnp.zeros_like(field[..., :1])], axis=-1)


def loss_sums(spectrum, total):
    harmonics = total // 2
    real_part = spectrum[:harmonics]
    imag_part = spectrum[harmonics:]
    power = (real_part * real_part + imag_part * imag_part) * (2.0 / total) ** 2
    freq = (jnp.arange(1, harmonics + 1, dtype=jnp.int32).astype(jnp.float32) / harmonics).reshape(-1, 1, 1, 1)
    root = jnp.sqrt(power)
    terms = (freq * power, (freq * freq) * power, freq**1.5 * (root * jnp.sqrt(root)))
    return jnp.stack([jnp.sum(term, axis=0) for term in terms], axis=0)


def by_cell(states):
    count = len(states)
    (packed,) = call(columns_kernel, [shape(LINE * count * 4 * ROWS, CZ)], [], 0, *states)
    packed = lax.all_to_all(packed.reshape(LINE, count, 4, ROWS, CZ), "tm", 0, 0, tiled=True)
    return packed.reshape(LINE * count, 4, ROWS, CZ)


def iteration(slice_start, conductivity, coil_current, switching, loss_coeffs):
    total = STEPS * LINE
    block = jnp.asarray(BLOCK_OF, jnp.int32)[lax.axis_index("mesh")]
    info = jnp.concatenate([jnp.stack([block, block % 2, lax.axis_index("tm")]), switching]).astype(jnp.int32)

    fields = gathered_copies(
        pack_kernel, shape(LINE, 4, 3, ROWS, CZ), 3 * LINE, conductivity, coil_current, slice_start[0]
    )
    packed = lax.all_to_all(fields, "mesh", 0, 0, tiled=True)

    packed = packed.reshape(LINE * 4 * 3 * ROWS, CZ)

    edge_rows = S_HALO + 2 * FINE_HALO
    cond, coil, start, edge_i, edge_x = call(
        unpack_kernel, [tile(), tile(), tile(), tile(edge_rows), tile(edge_rows)], [], 0, info, packed
    )
    rows = ROWS + 2 * FINE_HALO
    halo_i, halo_x = first_i, first_x = swap_halos(edge_i, edge_x)
    state, edge_i, edge_x, cond_all, coil_all = call(
        first_kernel,
        [tile(), tile(FINE_HALO), tile(FINE_HALO), tile(ROWS + 2 * S_HALO), tile(rows)],
        [rows] * 3,
        20 * SWEEPS * rows * NX * CZ,
        info,
        cond,
        coil,
        start,
        halo_i,
        halo_x,
    )

    def coarse(power, height, halo_at, value, halo_i, halo_x, edges=0):
        rows = ROWS + 2 * height
        return call(
            functools.partial(coarse_kernel, power, height, halo_at),
            [tile()] + [tile()] * edges,
            [rows] * 3,
            20 * CSWEEPS * power * rows * NX * CZ,
            info,
            cond_all,
            value,
            halo_i,
            halo_x,
        )

    (coarse_start,) = coarse(1, FINE_HALO, S_HALO + FINE_HALO, start, first_i, first_x)
    states = [state]
    for step in range(1, STEPS):
        halo_i, halo_x = swap_halos(edge_i, edge_x)
        if step == STEPS - 1:
            early = by_cell(states)
        state, edge_i, edge_x = call(
            functools.partial(fine_kernel, 0, step),
            [tile(), tile(FINE_HALO), tile(FINE_HALO)],
            [rows] * 3,
            20 * SWEEPS * rows * NX * CZ,
            info,
            cond_all,
            coil_all,
            state,
            halo_i,
            halo_x,
        )
        states.append(state)
    value, edge_i, edge_x = call(functools.partial(jump_kernel, ROWS), [tile()] * 3, [], 0, info, state, coarse_start)
    moved = 0
    for level, distance in enumerate(DISTANCES):
        halo_i, halo_x = swap_halos(edge_i, edge_x)
        arrived = earlier(value, distance)
        height = min(2 * distance, ROWS)
        product, power = value, distance
        if distance == 8:
            product, edge_i, edge_x = coarse(4, ROWS, 0, value, halo_i, halo_x, edges=2)
            halo_i, halo_x = swap_halos(edge_i, edge_x)
            power = 4
        (product,) = coarse(power, height, 0, product, halo_i, halo_x)
        if level + 1 < len(DISTANCES):
            next_height = min(2 * DISTANCES[level + 1], ROWS)
            value, edge_i, edge_x = call(
                functools.partial(combine_kernel, next_height, distance, moved),
                [tile(), tile(next_height), tile(next_height)],
                [],
                0,
                info,
                arrived,
                product,
            )
            if DISTANCES[level + 1] == 4:
                value, edge_i, edge_x, late, early = lax.optimization_barrier(
                    (value, edge_i, edge_x, states[-1], early)
                )
        moved += distance

    final = by_cell([late])
    table = dft_table(jnp.arange(total, dtype=jnp.int32), total, total // 2).reshape(total, LINE, STEPS)
    first_steps = table[:, :, : STEPS - 1].reshape(total, -1)
    spectrum = jnp.einsum("kt,txyz->kxyz", first_steps, z_difference(early), precision=lax.Precision.HIGHEST)
    last_step = table[:, :, STEPS - 1]
    spectrum += jnp.einsum("kt,txyz->kxyz", last_step, z_difference(final), precision=lax.Precision.HIGHEST)
    sums = loss_sums(spectrum, total)

    arrived, sums = lax.optimization_barrier((arrived, sums))
    (out,) = call(
        functools.partial(final_kernel, DISTANCES[-1], moved - DISTANCES[-1]),
        [shape(NX * ROWS, CZ)],
        [],
        0,
        info,
        arrived,
        product,
    )
    out = lax.all_to_all(out.reshape(LINE, 4, ROWS, CZ), "mesh", 0, 0, tiled=True)
    route = [(m * LINE + t, t * LINE + BLOCK_OF[m]) for m in range(LINE) for t in range(LINE)]
    sums = lax.ppermute(sums, ("mesh", "tm"), route)
    loss_density = jnp.sum(loss_coeffs * sums, axis=0)
    (next_start,) = call(lay_out_kernel, [shape(1, 4, LINE * ROWS, CZ)], [], 0, out)
    return next_start, loss_density


def solution(mesh):
    placed = (
        P("tm", "mesh", None, None),
        P("mesh", None, None),
        P("mesh", None, None),
        P("tm"),
        P(None, "mesh", "tm", None),
    )
    return jax.shard_map(
        iteration,
        mesh=mesh,
        in_specs=placed,
        out_specs=(P("tm", "mesh", None, None), P("mesh", "tm", None)),
        check_vma=False,
    )
```

```python
import functools

import jax
import jax.numpy as jnp
import numpy as np
from jax import lax
from jax.experimental import pallas as pl
from jax.experimental.pallas import tpu as pltpu
from jax.sharding import PartitionSpec as P


STEPS = 4
SWEEPS = 5
CSWEEPS = 2
TAU = 0.25
LINE = 16
ROWS = 8
NX = 64
CZ = 128
FINE_HALO = 5
S_HALO = 8
DISTANCES = (1, 2, 4, 8)

CHIP = [c if c < 4 else 11 - c for c in range(8)]
BLOCK_OF = [2 * CHIP[m // 2] + m % 2 for m in range(LINE)]
HOLDER = [BLOCK_OF.index(q) for q in range(LINE)]


def sweep_constants(scale, sweeps):
    upper = 2.0 + 12.0 * scale
    center = (upper + 0.5) / 2.0
    radius = (upper - 0.5) / 2.0
    ratio = center / radius
    weight = 1.0 / ratio
    pairs = []
    for _ in range(sweeps):
        weight_next = 1.0 / (2.0 * ratio - weight)
        pairs.append((weight_next * weight, 2.0 * weight_next / radius))
        weight = weight_next
    return 1.0 / center, pairs


def near_sum(now, row):
    row_id = lax.broadcasted_iota(jnp.int32, (NX, CZ), 0)
    lane_id = lax.broadcasted_iota(jnp.int32, (NX, CZ), 1)
    x = now[row]
    near = now[row - 1] + now[row + 1]
    near = near + jnp.where(row_id == 0, 0.0, pltpu.roll(x, 1, 0))
    near = near + jnp.where(row_id == NX - 1, 0.0, pltpu.roll(x, NX - 1, 0))
    near = near + jnp.where(lane_id == 0, 0.0, pltpu.roll(x, 1, 1))
    near = near + jnp.where(lane_id == CZ - 1, 0.0, pltpu.roll(x, CZ - 1, 1))
    return x, near


def solve(block, height, lo, hi, cond_at, rhs, a, b, scale, sweeps, store):
    inverse, pairs = sweep_constants(scale, sweeps)
    low = jnp.where(block > 0, 1.0, 0.0)
    high = jnp.where(block < LINE - 1, 1.0, 0.0)
    old, now = None, None
    for k, (alpha, beta) in enumerate(pairs):
        own = 1.0 + alpha - 6.0 * scale * beta
        unit = inverse if k == 0 else 1.0
        target = (a, b)[k % 2]
        for row in range(lo + k + 1, hi - k - 1):
            gain = unit * beta * scale
            if row < height:
                gain = gain * low
            elif row >= height + ROWS:
                gain = gain * high
            if k == 0:
                x, near = near_sum(rhs, row)
                new = x * ((inverse * own + beta) - (inverse * beta) * cond_at(row)) + gain * near
            else:
                x, near = near_sum(now, row)
                new = x * (own - beta * cond_at(row)) + gain * near
                if k == 1:
                    new = new + (beta - alpha * inverse) * rhs[row]
                else:
                    new = new + beta * rhs[row] - alpha * old[row]
            if k == sweeps - 1:
                store(row, new)
            else:
                target[row] = new
        old, now = now, target


def write_edges(parity, source, at, height, out_i, out_x):
    top = ROWS - height
    from_i = jnp.where(parity == 0, top, 0)
    out_i[...] = source[pl.ds(at + from_i, height)]
    out_x[...] = source[pl.ds(at + top - from_i, height)]


def places(parity, height):
    far = height + ROWS
    place_i = jnp.where(parity == 0, far, 0)
    return place_i, far - place_i


def pack_kernel(cond, coil, start, out, sems):
    copies = []
    for place, field in enumerate((cond, coil, start)):
        for m in range(LINE):
            copies.append(
                pltpu.make_async_copy(
                    field.at[:, pl.ds(BLOCK_OF[m] * ROWS, ROWS), :], out.at[m, :, place], sems.at[place * LINE + m]
                )
            )
    for copy in copies:
        copy.start()
    for copy in copies:
        copy.wait()


def unpack_kernel(info, packed, cond, coil, start, edge_i, edge_x):
    for row in range(ROWS):
        for place, out in enumerate((cond, coil, start)):
            out[row] = packed[pl.ds(place * ROWS + row, NX, stride=3 * ROWS), :]
    parity = info[1]
    at = 0
    for out, height in ((cond, S_HALO), (coil, FINE_HALO), (start, FINE_HALO)):
        write_edges(parity, out, 0, height, edge_i.at[pl.ds(at, height)], edge_x.at[pl.ds(at, height)])
        at += height


def gather_kernel(info, cond, coil, halo_i, halo_x, cond_all, coil_all):
    at = 0
    for own, target, height in ((cond, cond_all, S_HALO), (coil, coil_all, FINE_HALO)):
        place_i, place_x = places(info[1], height)
        target[pl.ds(height, ROWS)] = own[...]
        target[pl.ds(place_i, height)] = halo_i[pl.ds(at, height)]
        target[pl.ds(place_x, height)] = halo_x[pl.ds(at, height)]
        at += height


def first_kernel(info, cond, coil, own, halo_i, halo_x, state, edge_i, edge_x, cond_all, coil_all, a, b, rhs):
    gather_kernel(info, cond, coil, halo_i, halo_x, cond_all, coil_all)
    fine_kernel(
        S_HALO + FINE_HALO, 0, info, cond_all, coil_all, own, halo_i, halo_x, state, edge_i, edge_x, a, b, rhs
    )


def fine_kernel(halo_at, step, info, cond, coil, own, halo_i, halo_x, state, edge_i, edge_x, a, b, rhs):
    block, parity = info[0], info[1]
    height = FINE_HALO
    total = ROWS + 2 * height
    drive = TAU * info[3 + step].astype(jnp.float32)
    shift = S_HALO - height
    place_i, place_x = places(parity, height)
    for at, size, field, start in (
        (height, ROWS, own, 0),
        (place_i, height, halo_i, halo_at),
        (place_x, height, halo_x, halo_at),
    ):
        for row in range(size):
            rhs[at + row] = cond[at + row + shift] * field[start + row] + drive * coil[at + row]

    def store(row, value):
        state[row - height] = value

    solve(block, height, 0, total, lambda row: cond[row + shift], rhs, a, b, TAU, SWEEPS, store)
    if edge_i is not None:
        write_edges(parity, state, 0, height, edge_i, edge_x)


def last_kernel(info, cond, coil, own, halo_i, halo_x, coarse_start, state, value, edge_i, edge_x, a, b, rhs):
    fine_kernel(0, STEPS - 1, info, cond, coil, own, halo_i, halo_x, state, None, None, a, b, rhs)
    value[...] = state[...] - jnp.where(info[2] == LINE - 1, 0.0, 1.0) * coarse_start[...]
    write_edges(info[1], value, 0, 2 * DISTANCES[0], edge_i, edge_x)


def coarse_kernel(power, height, halo_at, edge_height, mix, info, cond, own, halo_i, halo_x, *rest):
    if mix:
        arrived, rest = rest[0], rest[1:]
        factor = reaches(info, *mix)
    outs, (a, b, c) = rest[:-3], rest[-3:]
    block, parity = info[0], info[1]
    scale = 4.0 * TAU
    shift = S_HALO - height
    place_i, place_x = places(parity, height)
    for at, size, field, start in (
        (height, ROWS, own, 0),
        (place_i, height, halo_i, halo_at),
        (place_x, height, halo_x, halo_at),
    ):
        for row in range(size):
            a[at + row] = cond[at + row + shift] * field[start + row]
    lo, hi = height - CSWEEPS * power, height + ROWS + CSWEEPS * power
    rhs, result = a, c
    for turn in range(power):
        if turn + 1 < power:

            def store(row, value, result=result):
                result[row] = cond[row + shift] * value

        else:

            def store(row, value):
                if mix:
                    value = arrived[row - height] + factor * value
                outs[0][row - height] = value

        solve(block, height, lo, hi, lambda row: cond[row + shift], rhs, b, None, scale, CSWEEPS, store)
        rhs, result = result, rhs
        lo, hi = lo + CSWEEPS, hi - CSWEEPS
    if len(outs) > 1:
        write_edges(parity, outs[0], 0, edge_height, outs[1], outs[2])


def reaches(info, distance, moved):
    position = lax.rem(info[2] + 1 + moved, LINE)
    return jnp.where(position + distance < LINE, 1.0, 0.0)


def combine_kernel(height, distance, moved, info, arrived, product, out, edge_i, edge_x):
    out[...] = arrived[...] + reaches(info, distance, moved) * product[...]
    write_edges(info[1], out, 0, height, edge_i, edge_x)


def columns_kernel(count, *refs):
    fields, out = refs[:count], refs[-1]
    for row in range(ROWS):
        for place, field in enumerate(fields):
            value = field[row]
            for m in range(LINE):
                first = (m * count + place) * (NX // LINE) * ROWS
                out[pl.ds(first + row, NX // LINE, stride=ROWS), :] = value[m * 4 : m * 4 + 4]


def final_kernel(distance, moved, info, arrived, product, out):
    factor = reaches(info, distance, moved)
    for row in range(ROWS):
        out[pl.ds(row, NX, stride=ROWS), :] = arrived[row] + factor * product[row]


def lay_out_kernel(blocks, out):
    for m in range(LINE):
        for x in range(NX // LINE):
            out[0, x, pl.ds(BLOCK_OF[m] * ROWS, ROWS), :] = blocks[m, x]


def gathered_copies(kernel, out, count, *args):
    return pl.pallas_call(
        kernel,
        out_shape=out,
        in_specs=[pl.BlockSpec(memory_space=pltpu.HBM)] * len(args),
        out_specs=pl.BlockSpec(memory_space=pltpu.VMEM),
        scratch_shapes=[pltpu.SemaphoreType.DMA((count,))],
        compiler_params=pltpu.CompilerParams(vmem_limit_bytes=60 << 20),
    )(*args)


def shape(*dims):
    return jax.ShapeDtypeStruct(dims, jnp.float32)


def tile(rows=ROWS):
    return shape(rows, NX, CZ)


def call(kernel, outs, scratch, flops, *args):
    size = sum(int(np.prod(o.shape)) for o in outs) + sum(int(np.prod(a.shape)) for a in args)
    spaces = [pltpu.SMEM if a.dtype == jnp.int32 else pltpu.VMEM for a in args]
    return pl.pallas_call(
        kernel,
        out_shape=outs,
        in_specs=[pl.BlockSpec(memory_space=space) for space in spaces],
        out_specs=[pl.BlockSpec(memory_space=pltpu.VMEM)] * len(outs),
        scratch_shapes=[pltpu.VMEM((rows, NX, CZ), jnp.float32) for rows in scratch],
        cost_estimate=pl.CostEstimate(flops=flops, bytes_accessed=4 * size, transcendentals=0),
        compiler_params=pltpu.CompilerParams(vmem_limit_bytes=24 << 20),
    )(*args)


def swap_halos(edge_i, edge_x):
    inner = [(m, m ^ 1) for m in range(LINE)]
    outer = []
    for q in range(1, LINE - 1, 2):
        outer += [(HOLDER[q], HOLDER[q + 1]), (HOLDER[q + 1], HOLDER[q])]
    halo_x = lax.ppermute(edge_x, "mesh", outer)
    halo_i = lax.ppermute(edge_i, "mesh", inner)
    return halo_i, halo_x


def earlier(value, distance):
    return lax.ppermute(value, "tm", [(n, (n - distance) % LINE) for n in range(LINE)])


def dft_table(sample_times, total, harmonics):
    orders = jnp.arange(1, harmonics + 1, dtype=jnp.int32)
    product = orders[:, None] * sample_times[None, :] % total
    angle = 2.0 * jnp.pi / total * product.astype(jnp.float32)
    return jnp.concatenate([jnp.cos(angle), -jnp.sin(angle)], axis=0)


def z_difference(field):
    inner = field[..., 1:] - field[..., :-1]
    return jnp.concatenate([inner, jnp.zeros_like(field[..., :1])], axis=-1)


def loss_sums(spectrum, total):
    harmonics = total // 2
    real_part = spectrum[:harmonics]
    imag_part = spectrum[harmonics:]
    power = (real_part * real_part + imag_part * imag_part) * (2.0 / total) ** 2
    freq = (jnp.arange(1, harmonics + 1, dtype=jnp.int32).astype(jnp.float32) / harmonics).reshape(-1, 1, 1, 1)
    root = jnp.sqrt(power)
    terms = (freq * power, (freq * freq) * power, freq**1.5 * (root * jnp.sqrt(root)))
    return jnp.stack([jnp.sum(term, axis=0) for term in terms], axis=0)


def by_cell(states, after=None):
    count = len(states)
    extra = () if after is None else (after,)
    (packed,) = call(functools.partial(columns_kernel, count), [shape(LINE * count * 4 * ROWS, CZ)], [], 0, *states, *extra)
    packed = lax.all_to_all(packed.reshape(LINE, count, 4, ROWS, CZ), "tm", 0, 0, tiled=True)
    return packed.reshape(LINE * count, 4, ROWS, CZ)


def iteration(slice_start, conductivity, coil_current, switching, loss_coeffs):
    total = STEPS * LINE
    block = jnp.asarray(BLOCK_OF, jnp.int32)[lax.axis_index("mesh")]
    info = jnp.concatenate([jnp.stack([block, block % 2, lax.axis_index("tm")]), switching]).astype(jnp.int32)

    fields = gathered_copies(
        pack_kernel, shape(LINE, 4, 3, ROWS, CZ), 3 * LINE, conductivity, coil_current, slice_start[0]
    )
    packed = lax.all_to_all(fields, "mesh", 0, 0, tiled=True)

    packed = packed.reshape(LINE * 4 * 3 * ROWS, CZ)

    edge_rows = S_HALO + 2 * FINE_HALO
    cond, coil, start, edge_i, edge_x = call(
        unpack_kernel, [tile(), tile(), tile(), tile(edge_rows), tile(edge_rows)], [], 0, info, packed
    )
    rows = ROWS + 2 * FINE_HALO
    halo_i, halo_x = first_i, first_x = swap_halos(edge_i, edge_x)
    state, edge_i, edge_x, cond_all, coil_all = call(
        first_kernel,
        [tile(), tile(FINE_HALO), tile(FINE_HALO), tile(ROWS + 2 * S_HALO), tile(rows)],
        [rows] * 3,
        20 * SWEEPS * rows * NX * CZ,
        info,
        cond,
        coil,
        start,
        halo_i,
        halo_x,
    )

    def coarse(power, height, halo_at, value, halo_i, halo_x, edge_height=0, mix=(), others=()):
        rows = ROWS + 2 * height
        return call(
            functools.partial(coarse_kernel, power, height, halo_at, edge_height, mix),
            [tile()] + [tile(edge_height)] * (2 if edge_height else 0),
            [rows] * 3,
            20 * CSWEEPS * power * rows * NX * CZ,
            info,
            cond_all,
            value,
            halo_i,
            halo_x,
            *others,
        )

    (coarse_start,) = coarse(1, FINE_HALO, S_HALO + FINE_HALO, start, first_i, first_x)
    states = [state]
    for step in range(1, STEPS):
        halo_i, halo_x = swap_halos(edge_i, edge_x)
        last = step == STEPS - 1
        if last:
            early = by_cell(states)
        results = call(
            last_kernel if last else functools.partial(fine_kernel, 0, step),
            [tile(), tile()] + [tile(2 * DISTANCES[0])] * 2 if last else [tile(), tile(FINE_HALO), tile(FINE_HALO)],
            [rows] * 3,
            20 * SWEEPS * rows * NX * CZ,
            info,
            cond_all,
            coil_all,
            state,
            halo_i,
            halo_x,
            *((coarse_start,) if last else ()),
        )
        if last:
            state, value, edge_i, edge_x = results
        else:
            state, edge_i, edge_x = results
            states.append(state)

    moved = 0
    for level, distance in enumerate(DISTANCES):
        halo_i, halo_x = swap_halos(edge_i, edge_x)
        arrived = earlier(value, distance)
        height = min(2 * distance, ROWS)
        product, power = value, distance
        if distance == 2:
            final = by_cell([state], early[:1, 0])
        if distance == 8:
            product, edge_i, edge_x = coarse(4, ROWS, 0, value, halo_i, halo_x, ROWS)
            halo_i, halo_x = swap_halos(edge_i, edge_x)
            power = 4
        (product,) = coarse(power, height, 0, product, halo_i, halo_x)
        if level + 1 < len(DISTANCES):
            next_height = min(2 * DISTANCES[level + 1], ROWS)
            value, edge_i, edge_x = call(
                functools.partial(combine_kernel, next_height, distance, moved),
                [tile(), tile(next_height), tile(next_height)],
                [],
                0,
                info,
                arrived,
                product,
            )
        moved += distance

    table = dft_table(jnp.arange(total, dtype=jnp.int32), total, total // 2).reshape(total, LINE, STEPS)
    first_steps = table[:, :, : STEPS - 1].reshape(total, -1)
    spectrum = jnp.einsum("kt,txyz->kxyz", first_steps, z_difference(early), precision=lax.Precision.HIGHEST)
    last_step = table[:, :, STEPS - 1]
    spectrum += jnp.einsum("kt,txyz->kxyz", last_step, z_difference(final), precision=lax.Precision.HIGHEST)
    sums = loss_sums(spectrum, total)

    route = [(m * LINE + t, t * LINE + BLOCK_OF[m]) for m in range(LINE) for t in range(LINE)]
    sums = lax.ppermute(sums, ("mesh", "tm"), route)
    (out,) = call(
        functools.partial(final_kernel, DISTANCES[-1], moved - DISTANCES[-1]),
        [shape(NX * ROWS, CZ)],
        [],
        0,
        info,
        arrived,
        product,
    )
    out = lax.all_to_all(out.reshape(LINE, 4, ROWS, CZ), "mesh", 0, 0, tiled=True)
    loss_density = jnp.sum(loss_coeffs * sums, axis=0)
    (next_start,) = call(lay_out_kernel, [shape(1, 4, LINE * ROWS, CZ)], [], 0, out)
    return next_start, loss_density


def solution(mesh):
    placed = (
        P("tm", "mesh", None, None),
        P("mesh", None, None),
        P("mesh", None, None),
        P("tm"),
        P(None, "mesh", "tm", None),
    )
    return jax.shard_map(
        iteration,
        mesh=mesh,
        in_specs=placed,
        out_specs=(P("tm", "mesh", None, None), P("mesh", "tm", None)),
        check_vma=False,
    )
```
